32 devices in a mesh: parts: 2 (over x), seq: 16 (over z, y, core).
Axes of the slice: x: 2, y: 2, z: 4, core: 2. Of those that a mesh axis runs over, the one named last changes fastest.
Arguments:
- queries: bfloat16 [2, 4, 8192], P(None, 'parts'), parts along dimension 1, may hold values from -7 to 7
- cache_k: bfloat16 [65536, 1024], P(('parts', 'seq')), parts along dimension 0, may hold values from -15 to 15
- cache_v: bfloat16 [65536, 1024], P(('parts', 'seq')), parts along dimension 0, may hold values from -6 to 6
- context_len: int32 [4], P('parts'), parts along dimension 0, may hold values from 8192 to 16384, as said below
- slot_seq: int32 [65536], P(('parts', 'seq')), parts along dimension 0, may hold values from 0 to 2, as said below
- slot_pos: int32 [65536], P(('parts', 'seq')), parts along dimension 0, may hold values from 0 to 16383, as said below
Outputs:
- attended: bfloat16 [2, 4, 8192], P(None, 'parts'), parts along dimension 1
The draws below stay inside these ranges and needn't reach their ends.
There are 2 independent parts, one for each index of `parts`. The reference program is written for one: setup_inputs(seed, part) draws one part's arguments, and reference() takes and returns one part's arrays. A program takes and returns all parts, laid end to end along the dimension named above; each array names one. Nothing has to cross between parts.
Inputs may be any that keep to these rules, and one draw needn't show every extreme that they name: Each sequence s has exactly context_len[s] slots with slot_seq = s; some sequence has exactly 16384. `slot_seq`: aligned blocks of 128 slots belong to one sequence or are free; the slots of a sequence hold each position from 0 to context_len[s] - 1 exactly once; free slots carry 2. `slot_pos`: 0 on free slots.
All inputs are finite; a program needn't handle non-finite values.
Results may differ from the reference program's by a relative error of at most 0.006.
Values may be sent and summed in bfloat16 or wider, within the bound.
A program may use at most 64 MiB of HBM per device.

```python
import jax
import jax.numpy as jnp
from jax import lax

QH = 64
KVH = 8
HD = 128
GROUP = 8
SEQS = 2
SLOT_DEV = 2048
BLOCK = 128
SLOTS = 32768
LEN_MAX = 16384
LEN_MIN = 8192
N_SEQ = 16


def cache_layout(key):
    base = jax.random.fold_in(key, 7)
    first_key, second_key, third_key = jax.random.split(base, 3)
    drawn = jax.random.randint(first_key, (SEQS,), LEN_MIN, LEN_MAX + 1).astype(jnp.int32)
    longest = jax.random.randint(third_key, (), 0, SEQS).astype(jnp.int32)
    seq_range = jnp.arange(SEQS, dtype=jnp.int32)
    lengths = jnp.where(seq_range == longest, jnp.int32(LEN_MAX), drawn).astype(jnp.int32)
    needed = (lengths + BLOCK - 1) // BLOCK
    block_ends = jnp.cumsum(needed)
    block_starts = block_ends - needed
    block_count = SLOTS // BLOCK
    shuffle = jax.random.permutation(second_key, block_count).astype(jnp.int32)
    rank_ids = jnp.arange(block_count, dtype=jnp.int32)
    owners = jnp.sum((rank_ids[:, None] >= block_ends[None, :]).astype(jnp.int32), axis=1)
    clipped = jnp.minimum(owners, SEQS - 1)
    within = rank_ids - block_starts[clipped]
    owner_phys = jnp.zeros((block_count,), jnp.int32).at[shuffle].set(owners)
    within_phys = jnp.zeros((block_count,), jnp.int32).at[shuffle].set(within)
    slot_ids = jnp.arange(SLOTS, dtype=jnp.int32)
    block_ids = slot_ids // BLOCK
    seq_of = owner_phys[block_ids]
    pos_of = within_phys[block_ids] * BLOCK + slot_ids % BLOCK
    length_of = lengths[jnp.minimum(seq_of, SEQS - 1)]
    valid = (seq_of < SEQS) & (pos_of < length_of)
    seq_of = jnp.where(valid, seq_of, SEQS).astype(jnp.int32)
    pos_of = jnp.where(valid, pos_of, 0).astype(jnp.int32)
    return (lengths, seq_of, pos_of)


def draw_context_len(key, part):
    return cache_layout(key)[0]


def draw_slot_seq(key, part):
    return cache_layout(key)[1]


def draw_slot_pos(key, part):
    return cache_layout(key)[2]


def draw_cache_k(key, part):
    own_key = jax.random.fold_in(key, 23)
    keys_out = jnp.clip(2.5 * jax.random.normal(own_key, (SLOTS, KVH * HD), jnp.float32), -15.0, 15.0)
    return keys_out.astype(jnp.bfloat16)


def draw_queries(key, part):
    own_key = jax.random.fold_in(key, 31)
    query_out = jnp.clip(jax.random.normal(own_key, (2, SEQS, QH, HD), jnp.float32), -6.0, 6.0)
    return query_out.reshape(2, SEQS, QH * HD).astype(jnp.bfloat16)


def level_of(stream_key, shape, shards, smallest, high):
    def one(position, shards_of):
        draws = jax.random.uniform(jax.random.fold_in(jax.random.fold_in(stream_key, 6), position), (shards_of,), jnp.float32, smallest / len(shards), high / len(shards))
        return jnp.repeat(jnp.exp(draws), shape[position] // shards_of).reshape((-1,) + (1,) * (len(shape) - position - 1))

    factor_of = one(*shards[0])
    for cut in shards[1:]:
        factor_of = factor_of * one(*cut)
    return factor_of


def scatter_about(rng, dims, deviation, limit, cuts=(), kind=jnp.bfloat16):
    entries = jax.random.normal(rng, dims, jnp.float32) * deviation
    if len(cuts) > 0:
        entries = level_of(rng, dims, cuts, -0.22, 0.18) * entries
    return jnp.clip(entries, min=-limit, max=limit).astype(kind)


def setup_inputs(seed: int = 0, part: int = 0) -> dict:
    seeds = jax.random.split(jax.random.key(seed), 7)
    part_splits = jax.random.split(jax.random.fold_in(seeds[6], part), 7)
    return {
        "queries": draw_queries(jax.random.fold_in(jax.random.fold_in(seeds[6], part), 71), part),
        "cache_k": draw_cache_k(jax.random.fold_in(jax.random.fold_in(seeds[6], part), 71), part),
        "cache_v": scatter_about(part_splits[2], (SLOTS, KVH * HD), 1.0, 6.0, ((0, 16),)),
        "context_len": draw_context_len(jax.random.fold_in(jax.random.fold_in(seeds[6], part), 71), part),
        "slot_seq": draw_slot_seq(jax.random.fold_in(jax.random.fold_in(seeds[6], part), 71), part),
        "slot_pos": draw_slot_pos(jax.random.fold_in(jax.random.fold_in(seeds[6], part), 71), part),
    }


def visible_slots(seq_block, pos_block, context_len):
    seq_ids = jnp.arange(SEQS, dtype=jnp.int32)
    step_ids = jnp.arange(2, dtype=jnp.int32)
    owners = seq_block[None, :] == seq_ids[:, None]
    last_visible = context_len[None, :] - 2 + step_ids[:, None]
    allowed = owners[None, :, :] & (pos_block[None, None, :] <= last_visible[:, :, None])
    return allowed[:, :, None, None, :]


def block_scores(query_heads, key_block):
    key_rows = key_block.astype(jnp.float32).reshape(SLOT_DEV, KVH, HD)
    scores = jnp.einsum('tsghd,ngd->tsghn', query_heads, key_rows, precision=lax.Precision.HIGHEST)
    return scores * (HD ** -0.5)


def reference(queries, cache_k, cache_v, context_len, slot_seq, slot_pos):
    query_heads = queries.astype(jnp.float32).reshape(2, SEQS, KVH, GROUP, HD)
    key_blocks = cache_k.reshape(N_SEQ, SLOT_DEV, KVH * HD)
    value_blocks = cache_v.reshape(N_SEQ, SLOT_DEV, KVH * HD)
    seq_blocks = slot_seq.reshape(N_SEQ, SLOT_DEV)
    pos_blocks = slot_pos.reshape(N_SEQ, SLOT_DEV)

    def block_max(inputs):
        key_block, seq_block, pos_block = inputs
        scores = block_scores(query_heads, key_block)
        allowed = visible_slots(seq_block, pos_block, context_len)
        return jnp.max(jnp.where(allowed, scores, jnp.float32(-1e30)), axis=-1)

    highest = jnp.max(lax.map(block_max, (key_blocks, seq_blocks, pos_blocks)), axis=0)

    def accumulate(carry, inputs):
        denom, numer = carry
        key_block, value_block, seq_block, pos_block = inputs
        scores = block_scores(query_heads, key_block)
        allowed = visible_slots(seq_block, pos_block, context_len)
        weights = jnp.where(allowed, jnp.exp(scores - highest[..., None]), jnp.float32(0.0))
        denom = denom + jnp.sum(weights, axis=-1)
        rounded = lax.optimization_barrier(weights.astype(jnp.bfloat16)).astype(jnp.float32)
        value_rows = value_block.astype(jnp.float32).reshape(SLOT_DEV, KVH, HD)
        numer = numer + jnp.einsum('tsghn,ngd->tsghd', rounded, value_rows, precision=lax.Precision.HIGHEST)
        return (denom, numer), None

    start = (jnp.zeros((2, SEQS, KVH, GROUP), jnp.float32), jnp.zeros((2, SEQS, KVH, GROUP, HD), jnp.float32))
    (denom, numer), _ = lax.scan(accumulate, start, (key_blocks, value_blocks, seq_blocks, pos_blocks))
    attended = (numer / denom[..., None]).astype(jnp.bfloat16)
    return attended.reshape(2, SEQS, QH * HD)
```

```python
import functools

import jax
import jax.numpy as jnp
from jax import lax
from jax.experimental import pallas as pl
from jax.experimental.pallas import tpu as pltpu
from jax.sharding import PartitionSpec as P

KVH = 8
HD = 128
INNER = 4
SHIFT = HD ** (-0.5) * 1.4426950408889634
HIDDEN = -1e30
MESH = pl.DeviceIdType.MESH


def rows_to_columns(rows):
    return jnp.transpose(rows)


def scaled_sum(ml, numer_refs, count, rows, final):
    maxima = [ml(i)[0:1, :] for i in range(count)]
    denoms = [ml(i)[1:2, :] for i in range(count)]
    top = functools.reduce(jnp.maximum, maxima)
    factors = [jnp.exp2((m - top) * SHIFT) for m in maxima]
    denom = sum(f * d for f, d in zip(factors, denoms))
    if final:
        factors = [f / denom for f in factors]
    pad = -count % 8
    if pad:
        factors = factors + [jnp.zeros((pad, 128), jnp.float32)]
    columns = jnp.transpose(jnp.concatenate(factors, axis=0))
    numer = None
    for i in range(count):
        term = numer_refs(i) * columns[:rows, i : i + 1]
        numer = term if numer is None else numer + term
    return top, denom, numer


def kernel(
    n, ctx, q_ref, k_hbm, v_hbm, seq_ref, pos_ref, out_ref,
    kbuf, vbuf, qf, bias,
    num1, ml1, rnum1, rml1, num2, ml2, rnum2, rml2, fin,
    ksem, vsem, s1, s1m, r1, r1m, s2, s2m, r2, r2m, s3, r3,
):
    me = lax.axis_index("seq")
    outer_count = n // INNER
    inner = me % INNER
    outer = me // INNER
    y = inner // 2
    c = inner % 2
    owners = [inner, y * 2 + (1 - c), (1 - y) * 2 + c, (1 - y) * 2 + (1 - c)]
    order = [2, 3, 1, 0]
    heads_each = KVH // INNER
    width = heads_each * HD
    rows = q_ref.shape[0] * q_ref.shape[1] * (q_ref.shape[2] // HD // KVH)
    group = q_ref.shape[2] // HD // KVH
    seqs = q_ref.shape[1]
    block = heads_each * rows

    kcopies, vcopies = {}, {}
    for j in order:
        columns = pl.ds(pl.multiple_of(owners[j] * width, width), width)
        kcopies[j] = pltpu.make_async_copy(k_hbm.at[:, columns], kbuf.at[j], ksem.at[j])
        kcopies[j].start()
        vcopies[j] = pltpu.make_async_copy(v_hbm.at[:, columns], vbuf.at[j], vsem.at[j])
        vcopies[j].start()

    barrier = pltpu.get_barrier_semaphore()
    plane_peers = {j: outer * INNER + owners[j] for j in (1, 2, 3)}
    chain_peers = {k: ((outer + k) % outer_count) * INNER + inner for k in range(1, outer_count)}
    peers = list(plane_peers.values()) + list(chain_peers.values())
    for peer in peers:
        pl.semaphore_signal(barrier, inc=1, device_id={"seq": peer}, device_id_type=MESH)

    for t in range(2):
        for head in range(KVH * group):
            g, h = head // group, head % group
            base = g * rows + t * group * seqs + h * seqs
            qf[base : base + seqs, :] = q_ref[t, :, head * HD : (head + 1) * HD].astype(jnp.float32)

    slots = k_hbm.shape[0]
    row_ids = lax.broadcasted_iota(jnp.int32, (rows, 128), 0)
    row_seq = row_ids % seqs
    row_step = row_ids // (group * seqs)
    last = jnp.zeros((rows, 128), jnp.int32)
    for s in range(seqs):
        last = jnp.where(row_seq == s, ctx[s], last)
    last = last - 2 + row_step
    for b in range(slots // 128):
        cut = slice(b * 128, (b + 1) * 128)
        owner = jnp.broadcast_to(seq_ref[:, cut], (rows, 128))
        pos = jnp.broadcast_to(pos_ref[:, cut], (rows, 128))
        allowed = (owner == row_seq) & (pos <= last)
        bias[:, cut] = jnp.where(allowed, 0.0, HIDDEN)

    copies1 = []
    for step, j in enumerate(order):
        owner = owners[j]
        kcopies[j].wait()
        stats = []
        probs = []
        for e in range(heads_each):
            start = pl.multiple_of((owner * heads_each + e) * rows, rows)
            q = qf[pl.ds(start, rows), :].astype(jnp.bfloat16)
            scores = lax.dot_general(
                q, kbuf[j, :, e * HD : (e + 1) * HD], (((1,), (1,)), ((), ())),
                preferred_element_type=jnp.float32,
            ) + bias[...]
            m = jnp.max(scores, axis=-1, keepdims=True)
            w = jnp.exp2((scores - m) * SHIFT)
            l = jnp.sum(w, axis=-1, keepdims=True)
            probs.append(w.astype(jnp.bfloat16))
            stats.append((m, l))
        vcopies[j].wait()
        for e in range(heads_each):
            num1[j, e * rows : (e + 1) * rows, :] = jnp.dot(
                probs[e], vbuf[j, :, e * HD : (e + 1) * HD], preferred_element_type=jnp.float32
            ).astype(jnp.bfloat16)
        lane = lax.broadcasted_iota(jnp.int32, (rows, 128), 1)
        packed = [jnp.where(lane == 0, m, l) for m, l in stats]
        packed = packed + [jnp.zeros((128 - block, 128), jnp.float32)]
        ml1[j] = jnp.transpose(jnp.concatenate(packed, axis=0))[:8, :]
        if j:
            if step == 0:
                pl.semaphore_wait(barrier, len(peers))
            for src, dst, ss, rs in ((ml1, rml1, s1m, r1m), (num1, rnum1, s1, r1)):
                copy = pltpu.make_async_remote_copy(
                    src_ref=src.at[j], dst_ref=dst.at[j], send_sem=ss.at[j], recv_sem=rs.at[j],
                    device_id={"seq": plane_peers[j]}, device_id_type=MESH,
                )
                copy.start()
                copies1.append(copy)

    for copy in copies1:
        copy.wait_recv()
    top, denom, numer = scaled_sum(
        lambda i: rml1[i] if i else ml1[0],
        lambda i: (rnum1[i] if i else num1[0]).astype(jnp.float32),
        INNER, block, False,
    )
    ml2[...] = jnp.concatenate([top, denom, jnp.zeros((6, 128), jnp.float32)], axis=0)
    num2[...] = numer.astype(jnp.bfloat16)

    copies2 = []
    for k in range(1, outer_count):
        for src, dst, ss, rs in ((ml2, rml2, s2m, r2m), (num2, rnum2, s2, r2)):
            copy = pltpu.make_async_remote_copy(
                src_ref=src, dst_ref=dst.at[k], send_sem=ss.at[k], recv_sem=rs.at[k],
                device_id={"seq": chain_peers[k]}, device_id_type=MESH,
            )
            copy.start()
            copies2.append(copy)
    for copy in copies2:
        copy.wait_recv()
    _, _, attended = scaled_sum(
        lambda i: rml2[i] if i else ml2[...],
        lambda i: (rnum2[i] if i else num2[...]).astype(jnp.float32),
        outer_count, block, True,
    )
    fin[0] = attended.astype(jnp.bfloat16)

    copies3 = []
    for j in (2, 3, 1):
        copy = pltpu.make_async_remote_copy(
            src_ref=fin.at[0], dst_ref=fin.at[j], send_sem=s3.at[j], recv_sem=r3.at[j],
            device_id={"seq": plane_peers[j]}, device_id_type=MESH,
        )
        copy.start()
        copies3.append((j, copy))

    def place(j):
        for e in range(heads_each):
            for t in range(2):
                for h in range(group):
                    base = e * rows + t * group * seqs + h * seqs
                    start = pl.multiple_of(((owners[j] * heads_each + e) * group + h) * HD, HD)
                    out_ref[t, :, pl.ds(start, HD)] = fin[j, base : base + seqs, :]

    place(0)
    for j, copy in reversed(copies3):
        copy.wait_recv()
        place(j)
    for copy in copies1 + copies2 + [copy for _, copy in copies3]:
        copy.wait_send()


def per_device(n, queries, cache_k, cache_v, context_len, slot_seq, slot_pos):
    slots = cache_k.shape[0]
    seqs = queries.shape[1]
    heads = queries.shape[2] // HD
    rows = 2 * seqs * heads // KVH
    heads_each = KVH // INNER
    block = heads_each * rows
    outer = n // INNER
    vmem = pl.BlockSpec(memory_space=pltpu.VMEM)
    dma = pltpu.SemaphoreType.DMA
    return pl.pallas_call(
        functools.partial(kernel, n),
        out_shape=jax.ShapeDtypeStruct(queries.shape, jnp.bfloat16),
        in_specs=[
            pl.BlockSpec(memory_space=pltpu.SMEM), vmem,
            pl.BlockSpec(memory_space=pl.ANY), pl.BlockSpec(memory_space=pl.ANY), vmem, vmem,
        ],
        out_specs=vmem,
        scratch_shapes=[
            pltpu.VMEM((INNER, slots, heads_each * HD), jnp.bfloat16),
            pltpu.VMEM((INNER, slots, heads_each * HD), jnp.bfloat16),
            pltpu.VMEM((KVH * rows, HD), jnp.float32),
            pltpu.VMEM((rows, slots), jnp.float32),
            pltpu.VMEM((INNER, block, HD), jnp.bfloat16),
            pltpu.VMEM((INNER, 8, 128), jnp.float32),
            pltpu.VMEM((INNER, block, HD), jnp.bfloat16),
            pltpu.VMEM((INNER, 8, 128), jnp.float32),
            pltpu.VMEM((block, HD), jnp.bfloat16),
            pltpu.VMEM((8, 128), jnp.float32),
            pltpu.VMEM((outer, block, HD), jnp.bfloat16),
            pltpu.VMEM((outer, 8, 128), jnp.float32),
            pltpu.VMEM((INNER, block, HD), jnp.bfloat16),
            dma((INNER,)), dma((INNER,)),
            dma((INNER,)), dma((INNER,)), dma((INNER,)), dma((INNER,)),
            dma((outer,)), dma((outer,)), dma((outer,)), dma((outer,)),
            dma((INNER,)), dma((INNER,)),
        ],
        compiler_params=pltpu.CompilerParams(collective_id=0, has_side_effects=True),
    )(context_len, queries, cache_k, cache_v, slot_seq.reshape(1, slots), slot_pos.reshape(1, slots))


def solution(mesh):
    return jax.shard_map(
        functools.partial(per_device, mesh.shape["seq"]),
        mesh=mesh,
        in_specs=(
            P(None, "parts", None),
            P(("parts", "seq"), None),
            P(("parts", "seq"), None),
            P("parts"),
            P(("parts", "seq")),
            P(("parts", "seq")),
        ),
        out_specs=P(None, "parts", None),
        check_vma=False,
    )
```

```python
import functools

import jax
import jax.numpy as jnp
from jax import lax
from jax.experimental import pallas as pl
from jax.experimental.pallas import tpu as pltpu
from jax.sharding import PartitionSpec as P

KVH = 8
HD = 128
INNER = 4
LIMIT = 16 << 20
SHIFT = HD ** (-0.5) * 1.4426950408889634
HIDDEN = -1e30
MESH = pl.DeviceIdType.MESH


def rows_to_columns(rows):
    return jnp.transpose(rows)


def scaled_sum(ml, numer_refs, count, rows, final):
    maxima = [ml(i)[0:1, :] for i in range(count)]
    denoms = [ml(i)[1:2, :] for i in range(count)]
    top = functools.reduce(jnp.maximum, maxima)
    factors = [jnp.exp2((m - top) * SHIFT) for m in maxima]
    denom = sum(f * d for f, d in zip(factors, denoms))
    if final:
        factors = [f / denom for f in factors]
    pad = -count % 8
    if pad:
        factors = factors + [jnp.zeros((pad, 128), jnp.float32)]
    columns = jnp.transpose(jnp.concatenate(factors, axis=0))
    numer = None
    for i in range(count):
        term = numer_refs(i) * columns[:rows, i : i + 1]
        numer = term if numer is None else numer + term
    return top, denom, numer


def kernel(
    n, ctx_hbm, q_hbm, k_hbm, v_hbm, seq_hbm, pos_hbm, fin,
    ctx, q_ref, seq_ref, pos_ref, kbuf, vbuf, qf, bias,
    num1, ml1, rnum1, rml1, num2, ml2, rnum2, rml2, own,
    isem, ksem, vsem, s1, s1m, r1, r1m, s2, s2m, r2, r2m, s3, r3,
):
    me = lax.axis_index("seq")
    outer_count = n // INNER
    inner = me % INNER
    outer = me // INNER
    y = inner // 2
    c = inner % 2
    owners = [inner, y * 2 + (1 - c), (1 - y) * 2 + c, (1 - y) * 2 + (1 - c)]
    heads_each = KVH // INNER
    width = heads_each * HD
    rows = q_ref.shape[0] * q_ref.shape[1] * (q_ref.shape[2] // HD // KVH)
    group = q_ref.shape[2] // HD // KVH
    seqs = q_ref.shape[1]
    block = heads_each * rows

    barrier = pltpu.get_barrier_semaphore()
    plane_peers = {j: outer * INNER + owners[j] for j in (1, 2, 3)}
    chain_peers = {k: ((outer + k) % outer_count) * INNER + inner for k in range(1, outer_count)}
    peers = list(plane_peers.values()) + list(chain_peers.values())
    for peer in peers:
        pl.semaphore_signal(barrier, inc=1, device_id={"seq": peer}, device_id_type=MESH)

    inputs = []
    for i, (src, dst) in enumerate(((q_hbm, q_ref), (seq_hbm, seq_ref), (pos_hbm, pos_ref), (ctx_hbm, ctx))):
        copy = pltpu.make_async_copy(src, dst, isem.at[i])
        copy.start()
        inputs.append(copy)
    kcopies, vcopies = {}, {}
    for which, j in (("k", 2), ("k", 3), ("v", 2), ("k", 1), ("v", 3), ("k", 0), ("v", 1), ("v", 0)):
        columns = pl.ds(pl.multiple_of(owners[j] * width, width), width)
        src, dst, sem, kept = (k_hbm, kbuf, ksem, kcopies) if which == "k" else (v_hbm, vbuf, vsem, vcopies)
        kept[j] = pltpu.make_async_copy(src.at[:, columns], dst.at[j], sem.at[j])
        kept[j].start()

    for copy in inputs:
        copy.wait()

    for t in range(2):
        for head in range(KVH * group):
            g, h = head // group, head % group
            base = g * rows + t * group * seqs + h * seqs
            qf[base : base + seqs, :] = q_ref[t, :, head * HD : (head + 1) * HD].astype(jnp.float32)

    slots = k_hbm.shape[0]
    row_ids = lax.broadcasted_iota(jnp.int32, (rows, 128), 0)
    row_seq = row_ids % seqs
    row_step = row_ids // (group * seqs)
    last = jnp.zeros((rows, 128), jnp.int32)
    for s in range(seqs):
        last = jnp.where(row_seq == s, ctx[s], last)
    last = last - 2 + row_step
    for b in range(slots // 128):
        cut = slice(b * 128, (b + 1) * 128)
        owner = jnp.broadcast_to(seq_ref[:, cut], (rows, 128))
        pos = jnp.broadcast_to(pos_ref[:, cut], (rows, 128))
        allowed = (owner == row_seq) & (pos <= last)
        bias[:, cut] = jnp.where(allowed, 0.0, HIDDEN)

    copies1 = []
    waiting = {}
    lane = lax.broadcasted_iota(jnp.int32, (rows, 128), 1)

    def score(j):
        kcopies[j].wait()
        probs = []
        packed = []
        for e in range(heads_each):
            start = pl.multiple_of((owners[j] * heads_each + e) * rows, rows)
            q = qf[pl.ds(start, rows), :].astype(jnp.bfloat16)
            scores = lax.dot_general(
                q, kbuf[j, :, e * HD : (e + 1) * HD], (((1,), (1,)), ((), ())),
                preferred_element_type=jnp.float32,
            ) + bias[...]
            m = jnp.max(scores, axis=-1, keepdims=True)
            w = jnp.exp2((scores - m) * SHIFT)
            l = jnp.sum(w, axis=-1, keepdims=True)
            probs.append(w.astype(jnp.bfloat16))
            packed.append(jnp.where(lane == 0, m, l))
        packed = packed + [jnp.zeros((128 - block, 128), jnp.float32)]
        ml1[j] = jnp.transpose(jnp.concatenate(packed, axis=0))[:2, :]
        waiting[j] = probs

    def send1(src, dst, ss, rs, j):
        copy = pltpu.make_async_remote_copy(
            src_ref=src.at[j], dst_ref=dst.at[j], send_sem=ss.at[j], recv_sem=rs.at[j],
            device_id={"seq": plane_peers[j]}, device_id_type=MESH,
        )
        copy.start()
        copies1.append(copy)

    def gather(j):
        vcopies[j].wait()
        for e in range(heads_each):
            num1[j, e * rows : (e + 1) * rows, :] = jnp.dot(
                waiting[j][e], vbuf[j, :, e * HD : (e + 1) * HD], preferred_element_type=jnp.float32
            ).astype(jnp.bfloat16)
        if j:
            if j == 2:
                pl.semaphore_wait(barrier, len(peers))
            send1(ml1, rml1, s1m, r1m, j)
            send1(num1, rnum1, s1, r1, j)

    score(2)
    score(3)
    gather(2)
    score(1)
    gather(3)
    score(0)
    gather(1)
    gather(0)

    for copy in copies1:
        copy.wait_recv()
    top, denom, numer = scaled_sum(
        lambda i: rml1[i] if i else ml1[0],
        lambda i: (rnum1[i] if i else num1[0]).astype(jnp.float32),
        INNER, block, False,
    )
    ml2[...] = jnp.concatenate([top, denom], axis=0)
    num2[...] = numer.astype(jnp.bfloat16)

    copies2 = []
    for k in range(1, outer_count):
        for src, dst, ss, rs in ((ml2, rml2, s2m, r2m), (num2, rnum2, s2, r2)):
            copy = pltpu.make_async_remote_copy(
                src_ref=src, dst_ref=dst.at[k], send_sem=ss.at[k], recv_sem=rs.at[k],
                device_id={"seq": chain_peers[k]}, device_id_type=MESH,
            )
            copy.start()
            copies2.append(copy)
    for copy in copies2:
        copy.wait_recv()
    _, _, attended = scaled_sum(
        lambda i: rml2[i] if i else ml2[...],
        lambda i: (rnum2[i] if i else num2[...]).astype(jnp.float32),
        outer_count, block, True,
    )
    own[...] = attended.astype(jnp.bfloat16)

    copies3 = []
    for j in (2, 3, 1):
        copy = pltpu.make_async_remote_copy(
            src_ref=own, dst_ref=fin.at[inner], send_sem=s3.at[j], recv_sem=r3.at[j],
            device_id={"seq": plane_peers[j]}, device_id_type=MESH,
        )
        copy.start()
        copies3.append(copy)
    fin[inner] = own[...]
    for copy in copies3:
        copy.wait_recv()
    for copy in copies1 + copies2 + copies3:
        copy.wait_send()


def place(fin, out_ref):
    steps, seqs, _ = out_ref.shape
    block = fin.shape[1]
    heads = fin.shape[0] * block // (steps * seqs)
    group = heads // KVH
    for head in range(heads):
        g, h = head // group, head % group
        for t in range(steps):
            row = g * group * steps * seqs + t * group * seqs + h * seqs
            i, base = row // block, row % block
            out_ref[t, :, head * HD : (head + 1) * HD] = fin[i, base : base + seqs, :]


def per_device(n, queries, cache_k, cache_v, context_len, slot_seq, slot_pos):
    slots = cache_k.shape[0]
    seqs = queries.shape[1]
    heads = queries.shape[2] // HD
    rows = 2 * seqs * heads // KVH
    heads_each = KVH // INNER
    block = heads_each * rows
    outer = n // INNER
    vmem = pl.BlockSpec(memory_space=pltpu.VMEM)
    dma = pltpu.SemaphoreType.DMA
    anywhere = pl.BlockSpec(memory_space=pltpu.HBM)
    attended = pl.pallas_call(
        functools.partial(kernel, n),
        out_shape=jax.ShapeDtypeStruct((INNER, block, HD), jnp.bfloat16),
        in_specs=[anywhere] * 6,
        out_specs=vmem,
        scratch_shapes=[
            pltpu.SMEM((seqs,), jnp.int32),
            pltpu.VMEM(queries.shape, jnp.bfloat16),
            pltpu.VMEM((1, slots), jnp.int32),
            pltpu.VMEM((1, slots), jnp.int32),
            pltpu.VMEM((INNER, slots, heads_each * HD), jnp.bfloat16),
            pltpu.VMEM((INNER, slots, heads_each * HD), jnp.bfloat16),
            pltpu.VMEM((KVH * rows, HD), jnp.float32),
            pltpu.VMEM((rows, slots), jnp.float32),
            pltpu.VMEM((INNER, block, HD), jnp.bfloat16),
            pltpu.VMEM((INNER, 2, 128), jnp.float32),
            pltpu.VMEM((INNER, block, HD), jnp.bfloat16),
            pltpu.VMEM((INNER, 2, 128), jnp.float32),
            pltpu.VMEM((block, HD), jnp.bfloat16),
            pltpu.VMEM((2, 128), jnp.float32),
            pltpu.VMEM((outer, block, HD), jnp.bfloat16),
            pltpu.VMEM((outer, 2, 128), jnp.float32),
            pltpu.VMEM((block, HD), jnp.bfloat16),
            dma((4,)), dma((INNER,)), dma((INNER,)),
            dma((INNER,)), dma((INNER,)), dma((INNER,)), dma((INNER,)),
            dma((outer,)), dma((outer,)), dma((outer,)), dma((outer,)),
            dma((INNER,)), dma((INNER,)),
        ],
        compiler_params=pltpu.CompilerParams(collective_id=0, has_side_effects=True, vmem_limit_bytes=LIMIT),
    )(*[
        pltpu.with_memory_space_constraint(x, pltpu.HBM)
        for x in (context_len, queries, cache_k, cache_v, slot_seq.reshape(1, slots), slot_pos.reshape(1, slots))
    ])
    return pl.pallas_call(
        place,
        out_shape=jax.ShapeDtypeStruct(queries.shape, jnp.bfloat16),
        in_specs=[vmem],
        out_specs=vmem,
        compiler_params=pltpu.CompilerParams(vmem_limit_bytes=4 << 20),
    )(attended)


def solution(mesh):
    return jax.shard_map(
        functools.partial(per_device, mesh.shape["seq"]),
        mesh=mesh,
        in_specs=(
            P(None, "parts", None),
            P(("parts", "seq"), None),
            P(("parts", "seq"), None),
            P("parts"),
            P(("parts", "seq")),
            P(("parts", "seq")),
        ),
        out_specs=P(None, "parts", None),
        check_vma=False,
    )
```
